32 devices in a mesh: tint: 8 (over z, x), tsec: 4 (over y, core).
Axes of the slice: x: 2, y: 2, z: 4, core: 2. Of those that a mesh axis runs over, the one named last changes fastest.
Arguments:
- history: bfloat16 [16, 2, 128, 16, 128], P('tint', None, None, 'tsec'), may hold values from -6 to 6
- first_row: float32 [2, 128, 16, 128], P(None, None, 'tsec'), may hold values from -6 to 6
- hamiltonian: float32 [128, 128], replicated, may hold values from -0.5 to 0.5
- coupling: float32 [128, 128], replicated, may hold values from 0.001 to 0.01
- window_start: int32 [128], replicated, may hold values from 0 to 7
- block_time: int32 [8], P('tint'), may hold values from 0 to 7, each once
Outputs:
- last_row: float32 [2, 128, 16, 128], P(None, None, 'tsec')
The draws below stay inside these ranges and needn't reach their ends.
Inputs may be any that keep to these rules, and one draw needn't show every extreme that they name: `block_time`: each block number appears once.
All inputs are finite; a program needn't handle non-finite values.
Results may differ from the reference program's by a relative error of at most 0.0058.
Values may be sent and summed in bfloat16 or wider, within the bound.
No kernel may reach another device: no remote copies, remote signals or barrier semaphores. Data moves between devices by JAX's collectives and lax.ppermute only.
A program may use at most 64 MiB of HBM per device.

```python
import math
import jax
import jax.numpy as jnp
from jax import lax

N = 128
S_DEV = 2
STEPS = 1
NT = 16
N_TINT = 8


def place_ends(values, key, least, top_value):
    shape = values.shape
    index_at = [jax.random.randint(jax.random.fold_in(key, axis), (), 0, shape[axis]) for axis in range(len(shape))]
    values = values.at[tuple(index_at)].set(least)
    longest = shape.index(max(shape))
    index_at[longest] = (index_at[longest] + 1) % shape[longest]
    return values.at[tuple(index_at)].set(top_value)


def block_scale(stream_key, shape, split, low, high):
    def one(position, blocks):
        steps = jax.random.uniform(jax.random.fold_in(jax.random.fold_in(stream_key, 6), position), (blocks,), jnp.float32, low / len(split), high / len(split))
        return jnp.repeat(jnp.exp(steps), shape[position] // blocks).reshape((-1,) + (1,) * (len(shape) - position - 1))

    gain = one(*split[0])
    for cut in split[1:]:
        gain = gain * one(*cut)
    return gain


def gaussian(own_key, dims, deviation, reach, split=(), kind=jnp.bfloat16):
    drawn = deviation * jax.random.normal(own_key, dims, jnp.float32)
    if split:
        drawn = drawn * block_scale(own_key, dims, split, -0.22, 0.18)
    return jnp.clip(drawn, -reach, reach).astype(kind)


def setup_inputs(seed: int = 0) -> dict:
    splits = jax.random.split(jax.random.key(seed), 7)
    return {
        "history": gaussian(splits[0], (NT, 2, N, NT, N), 1.0, 6.0, ((0, 8), (3, 4))),
        "first_row": gaussian(splits[1], (2, N, NT, N), 1.0, 6.0, ((2, 4),), jnp.float32),
        "hamiltonian": gaussian(splits[2], (N, N), N ** -0.5, 0.5, (), jnp.float32),
        "coupling": jnp.clip(jnp.exp(jax.random.uniform(splits[3], (N, N), jnp.float32, math.log(0.001), math.log(0.01))), 0.001, 0.01),
        "window_start": place_ends(jax.random.randint(splits[4], (N,), 0, NT // 2), jax.random.fold_in(splits[4], 1), 0, (NT // 2) - 1).astype(jnp.int32),
        "block_time": jax.random.permutation(splits[5], N_TINT).astype(jnp.int32),
    }


def reference(history, first_row, hamiltonian, coupling, window_start, block_time):
    times = (S_DEV * block_time[:, None] + jnp.arange(S_DEV, dtype=jnp.int32)[None, :]).reshape(-1).astype(jnp.int32)
    live = (times[None, :] >= window_start[:, None]).astype(jnp.float32)
    history_window_real = history[:, 0].reshape(NT * N, NT * N)
    history_window_imag = history[:, 1].reshape(NT * N, NT * N)
    current = first_row
    for number in range(STEPS):
        rounded = current.astype(jnp.bfloat16)
        picked = jnp.take(rounded, times, axis=2).astype(jnp.float32)
        real_part = picked[0]
        imag_part = picked[1]
        factor = -coupling[:, None, :] * live[:, :, None] * (real_part * real_part + imag_part * imag_part)
        self_energy_real = (factor * real_part).astype(jnp.bfloat16).reshape(N, NT * N)
        self_energy_imag = (factor * imag_part).astype(jnp.bfloat16).reshape(N, NT * N)
        collision_integral_real = jnp.dot(self_energy_real, history_window_real, preferred_element_type=jnp.float32) - jnp.dot(self_energy_imag, history_window_imag, preferred_element_type=jnp.float32)
        collision_integral_imag = jnp.dot(self_energy_real, history_window_imag, preferred_element_type=jnp.float32) + jnp.dot(self_energy_imag, history_window_real, preferred_element_type=jnp.float32)
        flattened_real = current[0].reshape(N, NT * N)
        flattened_imag = current[1].reshape(N, NT * N)
        hamiltonian_green_real = jnp.dot(hamiltonian, flattened_real, precision=lax.Precision.HIGHEST)
        hamiltonian_green_imag = jnp.dot(hamiltonian, flattened_imag, precision=lax.Precision.HIGHEST)
        advanced_real = flattened_real + 0.25 * (hamiltonian_green_imag + collision_integral_imag)
        advanced_imag = flattened_imag - 0.25 * (hamiltonian_green_real + collision_integral_real)
        current = jnp.stack([advanced_real, advanced_imag]).reshape(2, N, NT, N)
    return current
```

```python
import math

import jax
import jax.numpy as jnp
from jax import lax
from jax.sharding import PartitionSpec as P


def from_root(x, axis, size, root):
    me = lax.axis_index(axis)
    bit = 1
    if size & (size - 1) == 0:
        while bit < size:
            other = lax.ppermute(x, axis, [(i, i ^ bit) for i in range(size)])
            x = jnp.where((root & bit) == (me & bit), x, other)
            bit *= 2
        return x
    mine = x
    for k in range(1, size):
        got = lax.ppermute(mine, axis, [(i, (i + k) % size) for i in range(size)])
        x = jnp.where((root + k) % size == me, got, x)
    return x


def shift_outer(x, axis, outer, inner, k):
    pairs = [
        (o * inner + n, (o + k) % outer * inner + n) for o in range(outer) for n in range(inner)
    ]
    return lax.ppermute(x, axis, pairs)


def shift_inner(x, axis, outer, inner, k):
    pairs = [
        (o * inner + n, o * inner + (n + k) % inner) for o in range(outer) for n in range(inner)
    ]
    return lax.ppermute(x, axis, pairs)


def sum_over(parts, axis, outer, inner):
    place = lax.axis_index(axis) // inner
    sent = parts.astype(jnp.bfloat16)
    total = lax.dynamic_index_in_dim(parts, place, 0, keepdims=False)
    order = sorted(range(1, outer), key=lambda k: -min(k, outer - k))
    for k in order:
        chunk = lax.dynamic_index_in_dim(sent, (place + k) % outer, 0, keepdims=False)
        total = total + shift_outer(chunk, axis, outer, inner, k).astype(jnp.float32)
    mine = total.astype(jnp.bfloat16)
    position = lax.axis_index(axis) % inner
    pieces = [mine] + [shift_inner(mine, axis, outer, inner, k) for k in range(1, inner)]
    if inner == 2:
        mine = (pieces[0].astype(jnp.float32) + pieces[1].astype(jnp.float32)).astype(jnp.bfloat16)
    else:
        ordered = jnp.stack(pieces)
        mine = sum(
            lax.dynamic_index_in_dim(ordered, (position - n) % inner, 0, keepdims=False).astype(
                jnp.float32
            )
            for n in range(inner)
        ).astype(jnp.bfloat16)
    gathered = {0: mine}
    for k in order:
        gathered[k] = shift_outer(mine, axis, outer, inner, k)
    ordered = jnp.stack([gathered[k] for k in range(outer)])
    return jnp.stack(
        [
            lax.dynamic_index_in_dim(ordered, (place - q) % outer, 0, keepdims=False)
            for q in range(outer)
        ]
    )


def shards(tint_size, tsec_size, history, first_row, hamiltonian, coupling, window_start, block_time):
    points, _, orbitals, second_time, _ = history.shape
    first = block_time[0] * points
    root = first // second_time
    offset = first % second_time
    times = first + jnp.arange(points, dtype=jnp.int32)
    live = (times[None, :] >= window_start[:, None]).astype(jnp.float32)
    piece = lax.dynamic_slice_in_dim(first_row, offset, points, 2).astype(jnp.bfloat16)
    owned = from_root(piece, "tsec", tsec_size, root).astype(jnp.float32)
    real_part, imag_part = owned[0], owned[1]
    factor = (
        -coupling[:, None, :] * live[:, :, None] * (real_part * real_part + imag_part * imag_part)
    )
    sr = (factor * real_part).astype(jnp.bfloat16)
    si = (factor * imag_part).astype(jnp.bfloat16)
    left = jnp.stack([jnp.stack([sr, -si], 2), jnp.stack([si, sr], 2)])
    left = left.reshape(2 * orbitals, points * 2 * orbitals)
    window = history.reshape(points * 2 * orbitals, second_time * orbitals)
    terms = jnp.dot(left, window, preferred_element_type=jnp.float32)
    inner = max(d for d in range(1, math.isqrt(tint_size) + 1) if tint_size % d == 0)
    outer = tint_size // inner
    parts = terms.reshape(2, outer, orbitals // outer, second_time * orbitals).swapaxes(0, 1)
    summed = sum_over(parts, "tint", outer, inner)
    summed = summed.swapaxes(0, 1).reshape(2, orbitals, second_time * orbitals).astype(jnp.float32)
    flat = first_row.reshape(2, orbitals, second_time * orbitals)
    hg_real = jnp.dot(hamiltonian, flat[0], precision=lax.Precision.HIGHEST)
    hg_imag = jnp.dot(hamiltonian, flat[1], precision=lax.Precision.HIGHEST)
    advanced_real = flat[0] + 0.25 * (hg_imag + summed[1])
    advanced_imag = flat[1] - 0.25 * (hg_real + summed[0])
    return jnp.stack([advanced_real, advanced_imag]).reshape(first_row.shape)


def solution(mesh):
    tint_size, tsec_size = mesh.shape["tint"], mesh.shape["tsec"]

    def step(*arrays):
        return shards(tint_size, tsec_size, *arrays)

    return jax.shard_map(
        step,
        mesh=mesh,
        in_specs=(
            P("tint", None, None, "tsec", None),
            P(None, None, "tsec", None),
            P(),
            P(),
            P(),
            P("tint"),
        ),
        out_specs=P(None, None, "tsec", None),
        check_vma=False,
    )
```

```python
import math

import jax
import jax.numpy as jnp
from jax import lax
from jax.sharding import PartitionSpec as P


def power_of_two(size):
    return size & (size - 1) == 0


def from_root(x, axis, size, root):
    me = lax.axis_index(axis)
    if power_of_two(size):
        bit = size // 2
        while bit:
            other = lax.ppermute(x, axis, [(i, i ^ bit) for i in range(size)])
            x = jnp.where((root & bit) == (me & bit), x, other)
            bit //= 2
        return x
    mine = x
    for k in range(1, size):
        got = lax.ppermute(mine, axis, [(i, (i + k) % size) for i in range(size)])
        x = jnp.where((root + k) % size == me, got, x)
    return x


def to(place, k, size):
    return place ^ k if power_of_two(size) else (place + k) % size


def slot(place, owner, size):
    return place ^ owner if power_of_two(size) else (place - owner) % size


def send_low(x, axis, outer, inner, k):
    pairs = [
        (o * inner + n, o * inner + to(n, k, inner)) for o in range(outer) for n in range(inner)
    ]
    return lax.ppermute(x, axis, pairs)


def send_high(x, axis, outer, inner, k):
    pairs = [
        (o * inner + n, to(o, k, outer) * inner + n) for o in range(outer) for n in range(inner)
    ]
    return lax.ppermute(x, axis, pairs)


def sum_over(parts, axis, outer, inner):
    index = lax.axis_index(axis)
    place, row = index % inner, index // inner
    sent = parts.astype(jnp.bfloat16)
    total = lax.dynamic_index_in_dim(parts, place, 0, keepdims=False)
    for k in range(1, inner):
        chunk = lax.dynamic_index_in_dim(sent, to(place, k, inner), 0, keepdims=False)
        total = total + send_low(chunk, axis, outer, inner, k).astype(jnp.float32)
    mine = total.astype(jnp.bfloat16)
    pieces = [mine] + [send_high(mine, axis, outer, inner, k) for k in range(1, outer)]
    if outer == 2:
        mine = (pieces[0].astype(jnp.float32) + pieces[1].astype(jnp.float32)).astype(jnp.bfloat16)
    else:
        ordered = jnp.stack(pieces)
        mine = sum(
            lax.dynamic_index_in_dim(ordered, slot(row, o, outer), 0, keepdims=False).astype(
                jnp.float32
            )
            for o in range(outer)
        ).astype(jnp.bfloat16)
    ordered = jnp.stack([mine] + [send_low(mine, axis, outer, inner, k) for k in range(1, inner)])
    return jnp.stack(
        [
            lax.dynamic_index_in_dim(ordered, slot(place, q, inner), 0, keepdims=False)
            for q in range(inner)
        ]
    )


def shards(tint_size, tsec_size, history, first_row, hamiltonian, coupling, window_start, block_time):
    points, _, orbitals, second_time, _ = history.shape
    first = block_time[0] * points
    root = first // second_time
    offset = first % second_time
    times = first + jnp.arange(points, dtype=jnp.int32)
    live = (times[None, :] >= window_start[:, None]).astype(jnp.float32)
    piece = lax.dynamic_slice_in_dim(first_row, offset, points, 2).astype(jnp.bfloat16)
    owned = from_root(piece, "tsec", tsec_size, root).astype(jnp.float32)
    real_part, imag_part = owned[0], owned[1]
    factor = (
        -coupling[:, None, :] * live[:, :, None] * (real_part * real_part + imag_part * imag_part)
    )
    sr = (factor * real_part).astype(jnp.bfloat16)
    si = (factor * imag_part).astype(jnp.bfloat16)
    left = jnp.stack([jnp.stack([sr, -si], 2), jnp.stack([si, sr], 2)])
    left = left.reshape(2 * orbitals, points * 2 * orbitals)
    window = history.reshape(points * 2 * orbitals, second_time * orbitals)
    terms = jnp.dot(left, window, preferred_element_type=jnp.float32)
    outer = max(d for d in range(1, math.isqrt(tint_size) + 1) if tint_size % d == 0)
    inner = tint_size // outer
    parts = terms.reshape(2, inner, orbitals // inner, second_time * orbitals).swapaxes(0, 1)
    summed = sum_over(parts, "tint", outer, inner)
    summed = summed.swapaxes(0, 1).reshape(2, orbitals, second_time * orbitals).astype(jnp.float32)
    flat = first_row.reshape(2, orbitals, second_time * orbitals)
    hg_real = jnp.dot(hamiltonian, flat[0], precision=lax.Precision.HIGHEST)
    hg_imag = jnp.dot(hamiltonian, flat[1], precision=lax.Precision.HIGHEST)
    advanced_real = flat[0] + 0.25 * (hg_imag + summed[1])
    advanced_imag = flat[1] - 0.25 * (hg_real + summed[0])
    return jnp.stack([advanced_real, advanced_imag]).reshape(first_row.shape)


def solution(mesh):
    tint_size, tsec_size = mesh.shape["tint"], mesh.shape["tsec"]

    def step(*arrays):
        return shards(tint_size, tsec_size, *arrays)

    return jax.shard_map(
        step,
        mesh=mesh,
        in_specs=(
            P("tint", None, None, "tsec", None),
            P(None, None, "tsec", None),
            P(),
            P(),
            P(),
            P("tint"),
        ),
        out_specs=P(None, None, "tsec", None),
        check_vma=False,
    )
```

```python
import functools
import math

import jax
import jax.numpy as jnp
from jax import lax
from jax.experimental import pallas as pl
from jax.experimental.pallas import tpu as pltpu
from jax.sharding import PartitionSpec as P

VMEM = pl.BlockSpec(memory_space=pltpu.VMEM)
SMEM = pl.BlockSpec(memory_space=pltpu.SMEM)
ANY = pl.BlockSpec(memory_space=pl.ANY)


def power_of_two(size):
    return size & (size - 1) == 0


def to(place, k, size):
    return place ^ k if power_of_two(size) else lax.rem(place + k, size)


def slot(place, owner, size):
    return place ^ owner if power_of_two(size) else (place - owner) % size


def send_low(x, axis, outer, inner, k):
    n = range(inner)
    target = [i ^ k if power_of_two(inner) else (i + k) % inner for i in n]
    pairs = [(o * inner + i, o * inner + target[i]) for o in range(outer) for i in n]
    return lax.ppermute(x, axis, pairs)


def send_high(x, axis, outer, inner, k):
    target = [o ^ k if power_of_two(outer) else (o + k) % outer for o in range(outer)]
    pairs = [(o * inner + i, target[o] * inner + i) for o in range(outer) for i in range(inner)]
    return lax.ppermute(x, axis, pairs)


def shape_of(rows, columns, kind):
    return jax.ShapeDtypeStruct((rows, columns), kind)


def room(mebibytes):
    return pltpu.CompilerParams(vmem_limit_bytes=mebibytes << 20)


def cost(flops, moved):
    return pl.CostEstimate(flops=flops, bytes_accessed=moved, transcendentals=0)


def piece_kernel(points, orbitals, second_time, block_ref, row_ref, piece_ref):
    groups = second_time // points
    block = block_ref[...]
    group = block & (groups - 1) if power_of_two(groups) else lax.rem(block, groups)
    for p in range(points):
        for part in range(2):
            start = part * orbitals * second_time + p
            rows = row_ref[pl.ds(start, orbitals, stride=second_time), :]
            for g in range(1, groups):
                here = pl.ds(start + g * points, orbitals, stride=second_time)
                rows = jnp.where(group == g, row_ref[here, :], rows)
            at = (p * 2 + part) * orbitals
            piece_ref[at : at + orbitals, :] = rows.astype(jnp.bfloat16)


def pick_kernel(points, second_time, bit, axis, block_ref, mine_ref, other_ref, out_ref):
    root = lax.div(block_ref[0] * points, second_time)
    mine = (root & bit) == (lax.axis_index(axis) & bit)

    @pl.when(mine)
    def _():
        out_ref[...] = mine_ref[...]

    @pl.when(jnp.logical_not(mine))
    def _():
        out_ref[...] = other_ref[...]


def ready_kernel(
    points, orbitals, second_time, inner, axis,
    block_ref, start_ref, coupling_ref, hamiltonian_ref, history_ref, row_ref,
    window_ref, scaled_ref, base_ref,
):
    n, width = orbitals, orbitals // inner
    place = lax.rem(lax.axis_index(axis), inner)
    first = block_ref[0] * points
    for k in range(inner):
        at = pl.multiple_of(to(place, k, inner) * width, width)
        rows = -coupling_ref[pl.ds(at, width), :]
        begins = start_ref[pl.ds(at, width), :]
        for p in range(points):
            live = (first + p >= begins).astype(jnp.float32)
            scaled_ref[(k * points + p) * width : (k * points + p + 1) * width, :] = rows * live
    for part in range(2):
        other = 1 - part
        now, turned = (
            jnp.concatenate(
                [
                    row_ref[pl.ds(which * n * second_time + t, n, stride=second_time), :]
                    for t in range(second_time)
                ],
                1,
            )
            for which in (part, other)
        )
        hg = jnp.dot(
            hamiltonian_ref[...],
            turned,
            precision=lax.Precision.HIGHEST,
            preferred_element_type=jnp.float32,
        )
        base_ref[part * n : (part + 1) * n, :] = now + 0.25 * hg if part == 0 else now - 0.25 * hg
    rows = points * 2 * n
    spread = history_ref[...].astype(jnp.float32).reshape(rows, second_time, n)
    for t in range(second_time):
        window_ref[:, t * n : (t + 1) * n] = spread[:, t, :].astype(jnp.bfloat16)


def terms_kernel(
    points, orbitals, second_time, bit, inner, tint, tsec,
    block_ref, mine_ref, other_ref, scaled_ref, window_ref, own_ref, *rest,
):
    *sent_refs, left = rest
    n, width = orbitals, orbitals // inner
    root = lax.div(block_ref[0] * points, second_time)
    mine = (root & bit) == (lax.axis_index(tsec) & bit)
    place = lax.rem(lax.axis_index(tint), inner)
    for k in range(inner):
        at = pl.multiple_of(to(place, k, inner) * width, width)
        low = k * 2 * width
        for p in range(points):
            real, imag = (
                jnp.where(
                    mine,
                    mine_ref[pl.ds((p * 2 + part) * n + at, width), :].astype(jnp.float32),
                    other_ref[pl.ds((p * 2 + part) * n + at, width), :].astype(jnp.float32),
                )
                for part in range(2)
            )
            scaled = scaled_ref[(k * points + p) * width : (k * points + p + 1) * width, :]
            factor = scaled * (real * real + imag * imag)
            sr, si = factor * real, factor * imag
            c = p * 2 * n
            left[low : low + width, c : c + n] = sr.astype(jnp.bfloat16)
            left[low : low + width, c + n : c + 2 * n] = (-si).astype(jnp.bfloat16)
            left[low + width : low + 2 * width, c : c + n] = si.astype(jnp.bfloat16)
            left[low + width : low + 2 * width, c + n : c + 2 * n] = sr.astype(jnp.bfloat16)
    product = jnp.dot(left[...], window_ref[...], preferred_element_type=jnp.float32)
    own_ref[...] = product[: 2 * width, :]
    for k in range(1, inner):
        sent_refs[k - 1][...] = product[k * 2 * width : (k + 1) * 2 * width, :].astype(jnp.bfloat16)


def update_kernel(orbitals, second_time, inner, axis, base_ref, *rest):
    *chunk_refs, out_ref, held, sem = rest
    n, width = orbitals, orbitals // inner
    place = lax.rem(lax.axis_index(axis), inner)
    copies = []
    for k in range(inner):
        owner = to(place, k, inner) if power_of_two(inner) else lax.rem(place - k + inner, inner)
        at = pl.multiple_of(owner * width, width)
        terms = chunk_refs[k][...].astype(jnp.float32)
        for part in range(2):
            base = base_ref[pl.ds(pl.multiple_of(part * n + at, width), width), :]
            if part == 0:
                new = base + 0.25 * terms[width:, :]
            else:
                new = base - 0.25 * terms[:width, :]
            start = pl.multiple_of((part * n + at) * second_time, width * second_time)
            for t in range(second_time):
                held[pl.ds(start + t, width, stride=second_time), :] = new[:, t * n : (t + 1) * n]
            rows = pl.ds(start, width * second_time)
            copy = pltpu.make_async_copy(held.at[rows], out_ref.at[rows], sem.at[2 * k + part])
            copy.start()
            copies.append(copy)
    for copy in copies:
        copy.wait()


def shards(tint_size, tsec_size, history, first_row, hamiltonian, coupling, window_start, block_time):
    points, _, n, second_time, _ = history.shape
    outer = max(d for d in range(1, math.isqrt(tint_size) + 1) if tint_size % d == 0)
    inner = tint_size // outer
    width = n // inner
    sizes = (points, n, second_time)
    rows = 2 * n * second_time
    flat = first_row.reshape(rows, n)
    piece = pl.pallas_call(
        functools.partial(piece_kernel, *sizes),
        out_shape=shape_of(points * 2 * n, n, jnp.bfloat16),
        in_specs=[VMEM, VMEM],
        out_specs=VMEM,
        compiler_params=room(8),
        cost_estimate=cost(0, 4 * rows * n),
    )(block_time.reshape(1, 1), flat)
    window, scaled, base = pl.pallas_call(
        functools.partial(ready_kernel, *sizes, inner, "tint"),
        out_shape=(
            shape_of(points * 2 * n, second_time * n, jnp.bfloat16),
            shape_of(points * n, n, jnp.float32),
            shape_of(2 * n, second_time * n, jnp.float32),
        ),
        in_specs=[SMEM] + [VMEM] * 5,
        out_specs=(VMEM, VMEM, VMEM),
        compiler_params=room(8),
        cost_estimate=cost(24 * n * n * n * second_time, 8 * rows * n),
    )(
        block_time,
        window_start.reshape(n, 1),
        coupling,
        hamiltonian,
        history.reshape(points * rows, n),
        flat,
    )
    bit = tsec_size // 2
    other, made = piece, None
    while bit:
        other = lax.ppermute(piece, "tsec", [(i, i ^ bit) for i in range(tsec_size)])
        if not made:
            other, *made = lax.optimization_barrier((other, window, scaled, base))
            window, scaled, base = made
        if bit == 1:
            break
        piece = pl.pallas_call(
            functools.partial(pick_kernel, points, second_time, bit, "tsec"),
            out_shape=shape_of(points * 2 * n, n, jnp.bfloat16),
            in_specs=[SMEM, VMEM, VMEM],
            out_specs=VMEM,
            compiler_params=room(8),
            cost_estimate=cost(0, 4 * points * n * n),
        )(block_time, piece, other)
        bit //= 2
    own, *sent = pl.pallas_call(
        functools.partial(terms_kernel, *sizes, bit, inner, "tint", "tsec"),
        out_shape=[shape_of(2 * width, second_time * n, jnp.float32)]
        + [shape_of(2 * width, second_time * n, jnp.bfloat16)] * (inner - 1),
        in_specs=[SMEM] + [VMEM] * 4,
        out_specs=[VMEM] * inner,
        scratch_shapes=[pltpu.VMEM((2 * n, points * 2 * n), jnp.bfloat16)],
        compiler_params=room(8),
        cost_estimate=cost(8 * points * n * n * n * second_time, 4 * rows * n),
    )(block_time, piece, other, scaled, window)
    total = own
    for k in range(1, inner):
        total = total + send_low(sent[k - 1], "tint", outer, inner, k).astype(jnp.float32)
    mine = total.astype(jnp.bfloat16)
    pieces = [mine] + [send_high(mine, "tint", outer, inner, k) for k in range(1, outer)]
    if outer == 2:
        mine = (pieces[0].astype(jnp.float32) + pieces[1].astype(jnp.float32)).astype(jnp.bfloat16)
    else:
        ordered = jnp.stack(pieces)
        high = lax.axis_index("tint") // inner
        mine = sum(
            lax.dynamic_index_in_dim(ordered, slot(high, o, outer), 0, keepdims=False).astype(
                jnp.float32
            )
            for o in range(outer)
        ).astype(jnp.bfloat16)
    chunks = [mine] + [send_low(mine, "tint", outer, inner, k) for k in range(1, inner)]
    new = pl.pallas_call(
        functools.partial(update_kernel, n, second_time, inner, "tint"),
        out_shape=shape_of(rows, n, jnp.float32),
        in_specs=[VMEM] * (1 + inner),
        out_specs=ANY,
        scratch_shapes=[
            pltpu.VMEM((rows, n), jnp.float32),
            pltpu.SemaphoreType.DMA((2 * inner,)),
        ],
        compiler_params=room(8),
        cost_estimate=cost(4 * rows * n, 8 * rows * n),
    )(base, *chunks)
    return new.reshape(first_row.shape)


def solution(mesh):
    tint_size, tsec_size = mesh.shape["tint"], mesh.shape["tsec"]

    def step(*arrays):
        return shards(tint_size, tsec_size, *arrays)

    return jax.shard_map(
        step,
        mesh=mesh,
        in_specs=(
            P("tint", None, None, "tsec", None),
            P(None, None, "tsec", None),
            P(),
            P(),
            P(),
            P("tint"),
        ),
        out_specs=P(None, None, "tsec", None),
        check_vma=False,
    )
```
